128 devices in a mesh: gy: 32 (over z, y, core), var: 4 (over x).
Axes of the slice: x: 4, y: 4, z: 4, core: 2. Of those that a mesh axis runs over, the one named last changes fastest.
Arguments:
- field: float32 [32, 32, 1024, 128], P('var', None, 'gy')
- factor_x: float32 [32, 16], replicated, may hold values from -1 to 1
- factor_y: float32 [1024, 64], P('gy'), may hold values from -0.1875 to 0.1875
- factor_z: float32 [128, 64], replicated, may hold values from -0.5 to 0.5
- factor_v: float32 [32, 16], replicated, may hold values from -1 to 1
Outputs:
- proj_z: float32 [128, 128], replicated
- proj_v: float32 [32, 32], replicated
- core_rms: float32 [], replicated
The draws below stay inside these ranges and needn't reach their ends.
All inputs are finite; a program needn't handle non-finite values.
Results may differ from the reference program's by a relative error of at most 0.0003.
Values sent between devices are 32-bit elements; how exact they have to be, the bound alone decides.
No kernel may reach another device: no remote copies, remote signals or barrier semaphores. Data moves between devices by JAX's collectives and lax.ppermute only.
A program may use at most 192 MiB of HBM per device.

```python
import jax
import jax.numpy as jnp
from jax import lax

NV = 32
NX = 32
NZ = 128
RX = 16
RY = 64
RZ = 64
RV = 16
NY = 1024


def draw_field(key, part):
    key_var, key_cell, key_base = jax.random.split(key, 3)
    low = jnp.log(0.3)
    high = jnp.log(3.0)
    var_scale = jnp.exp(jax.random.uniform(key_var, (NV,), jnp.float32, low, high))
    cell_scale = jnp.exp(jax.random.uniform(key_cell, (NY, NZ), jnp.float32, low, high))
    rising = 1.0 + 2.0 * jnp.arange(NY, dtype=jnp.float32) / NY
    base = jax.random.normal(key_base, (NV, NX, NY, NZ), jnp.float32)
    scale = rising[:, None] * cell_scale
    return var_scale[:, None, None, None] * scale[None, None, :, :] * base


def levels(rng, dims, cuts, low, largest):
    def one(axis_at, parts):
        heights = jax.random.uniform(jax.random.fold_in(jax.random.fold_in(rng, 6), axis_at), (parts,), jnp.float32, low / len(cuts), largest / len(cuts))
        return jnp.repeat(jnp.exp(heights), dims[axis_at] // parts).reshape((-1,) + (1,) * (len(dims) - axis_at - 1))

    loudness = one(*cuts[0])
    for cut in cuts[1:]:
        loudness = loudness * one(*cut)
    return loudness


def noise(rng, dims, spread, limit, pieces=(), kind=jnp.bfloat16):
    factor_of = levels(rng, dims, pieces, -0.22, 0.18) if pieces else 1.0
    result = jax.random.normal(rng, dims, jnp.float32) * spread * factor_of
    return jnp.minimum(jnp.maximum(result, -limit), limit).astype(kind)


def setup_inputs(seed: int = 0) -> dict:
    keys = jax.random.split(jax.random.key(seed), 6)
    return {
        "field": draw_field(jax.random.fold_in(keys[5], 71), 0),
        "factor_x": noise(keys[1], (NX, RX), NX ** -0.5, 1.0, (), jnp.float32),
        "factor_y": noise(keys[2], (NY, RY), NY ** -0.5, 0.1875, ((0, 32),), jnp.float32),
        "factor_z": noise(keys[3], (NZ, RZ), NZ ** -0.5, 0.5, (), jnp.float32),
        "factor_v": noise(keys[4], (NV, RV), NV ** -0.5, 1.0, (), jnp.float32),
    }


precise = lax.Precision.HIGHEST

def orth(mat):
    gram = jnp.dot(mat.T, mat, precision=precise)
    lower = jnp.linalg.cholesky(gram)
    return jax.scipy.linalg.solve_triangular(lower, mat.T, lower=True).T

def reference(field, factor_x, factor_y, factor_z, factor_v):
    along_x = jnp.einsum('vxyz,xa->vayz', field, factor_x, precision=precise)
    partial_value = jnp.einsum('vayz,yb->vabz', along_x, factor_y, precision=precise)
    wide_z = jnp.einsum('vabz,vc->cabz', partial_value, factor_v, precision=precise)
    small_core = jnp.einsum('cabz,zr->cabr', wide_z, factor_z, precision=precise)
    raw_z = jnp.einsum('cabz,cabr->zr', wide_z, small_core, precision=precise)
    new_z = orth(raw_z)
    proj_z = jnp.dot(new_z, new_z.T, precision=precise)
    wide_v = jnp.einsum('vabz,zr->vabr', partial_value, new_z, precision=precise)
    flat_v = wide_v.reshape(wide_v.shape[0], -1)
    gram_v = jnp.dot(flat_v, flat_v.T, precision=precise)
    new_v = orth(jnp.dot(gram_v, factor_v, precision=precise))
    proj_v = jnp.dot(new_v, new_v.T, precision=precise)
    core = jnp.dot(new_v.T, flat_v, precision=precise)
    core_rms = jnp.sqrt(jnp.mean(core * core))
    return (proj_z, proj_v, core_rms)
```

```python
import jax
import jax.numpy as jnp
from jax import lax
from jax.sharding import Mesh, PartitionSpec as P

precise = lax.Precision.HIGHEST


def orth(mat):
    gram = jnp.dot(mat.T, mat, precision=precise)
    lower = jnp.linalg.cholesky(gram)
    return jax.scipy.linalg.solve_triangular(lower, mat.T, lower=True).T


def shift(value, axis, step):
    return lax.ppermute(value, axis, [(i, (i + step) % 4) for i in range(4)])


def from_all(value, axes, count):
    copies = jnp.broadcast_to(value[None], (count,) + value.shape)
    return lax.all_to_all(copies, axes, 0, 0, tiled=True)


def per_device(field, factor_x, factor_y, factor_z, factor_v):
    core = lax.axis_index("c")
    swap = [(0, 1), (1, 0)]
    other_y = lax.ppermute(factor_y, "c", swap)
    along_x = jnp.einsum("vxyz,xa->avyz", field, factor_x, precision=precise)
    keep = lax.dynamic_slice_in_dim(along_x, core * 8, 8, 0)
    send = lax.dynamic_slice_in_dim(along_x, (1 - core) * 8, 8, 0)
    got = lax.ppermute(send, "c", swap)
    both = jnp.concatenate([keep, got], axis=2)
    both_y = jnp.concatenate([factor_y, other_y], axis=0)
    part = jnp.einsum("avyz,yb->avbz", both, both_y, precision=precise)
    part = part.reshape(8, 8, 8, 8, 128).transpose(0, 2, 1, 3, 4).reshape(64, 8, 8, 128)
    parts = lax.all_to_all(part, ("z", "y", "x"), 0, 0, tiled=True)
    block = parts.reshape(16, 4, 8, 8, 128).sum(0).reshape(32, 8, 128)

    wide_z = jnp.einsum("vbz,vc->cbz", block, factor_v, precision=precise).reshape(128, 128)
    small_core = jnp.dot(wide_z, factor_z, precision=precise)
    raw = jnp.dot(small_core.T, wide_z, precision=precise)
    raw = raw + lax.ppermute(raw, "c", swap)
    raw = from_all(raw, ("z", "y"), 16).sum(0)
    raw = raw + shift(raw, "x", 1) + (shift(raw, "x", 2) + shift(raw, "x", 3))
    new_z = orth(raw.T)
    proj_z = jnp.dot(new_z, new_z.T, precision=precise)

    wide_v = jnp.einsum("vbz,zr->bvr", block, new_z, precision=precise)
    gram_v = jnp.einsum("bvr,bwr->vw", wide_v, wide_v, precision=precise)
    gram_v = from_all(gram_v.reshape(8, 128), ("z", "y", "c", "x"), 128).sum(0).reshape(32, 32)
    new_v = orth(jnp.dot(gram_v, factor_v, precision=precise))
    proj_v = jnp.dot(new_v, new_v.T, precision=precise)
    total = jnp.sum(new_v * jnp.dot(gram_v, new_v, precision=precise))
    core_rms = jnp.sqrt(total / (16 * 16 * 64 * 64))
    return (proj_z, proj_v, core_rms)


def solution(mesh):
    fine = Mesh(mesh.devices.reshape(4, 4, 2, 4), ("z", "y", "c", "x"))
    rows = ("z", "y", "c")
    in_specs = (P("x", None, rows, None), P(), P(rows, None), P(), P())
    out_specs = (P(), P(), P())
    return jax.shard_map(
        per_device, mesh=fine, in_specs=in_specs, out_specs=out_specs, check_vma=False
    )
```

```python
import jax
import jax.numpy as jnp
from jax import lax
from jax.sharding import Mesh, PartitionSpec as P

precise = lax.Precision.HIGHEST


def orth(mat):
    gram = jnp.dot(mat.T, mat, precision=precise)
    lower = jnp.linalg.cholesky(gram)
    return jax.scipy.linalg.solve_triangular(lower, mat.T, lower=True).T


def from_all(value, axes, count):
    copies = jnp.broadcast_to(value[None], (count,) + value.shape)
    return lax.all_to_all(copies, axes, 0, 0, tiled=True)


def per_device(field, factor_x, factor_y, factor_z, factor_v):
    core = lax.axis_index("c")
    swap = [(0, 1), (1, 0)]
    other_y = lax.ppermute(factor_y, "c", swap)
    along_x = jnp.einsum("vxyz,xa->avyz", field, factor_x, precision=precise)
    keep = lax.dynamic_slice_in_dim(along_x, core * 8, 8, 0)
    send = lax.dynamic_slice_in_dim(along_x, (1 - core) * 8, 8, 0)
    got = lax.ppermute(send, "c", swap)
    both = jnp.concatenate([keep, got], axis=2)
    both_y = jnp.concatenate([factor_y, other_y], axis=0)
    part = jnp.einsum("avyz,yb->avbz", both, both_y, precision=precise)
    part = part.reshape(8, 8, 2, 32, 128).transpose(0, 2, 1, 3, 4).reshape(16, 8, 32, 128)
    parts = lax.all_to_all(part, ("z", "y"), 0, 0, tiled=True)
    block = from_all(parts.sum(0), "x", 4).reshape(32, 32, 128)

    wide_z = jnp.einsum("vbz,vc->cbz", block, factor_v, precision=precise).reshape(512, 128)
    small_core = jnp.dot(wide_z, factor_z, precision=precise)
    raw = jnp.dot(small_core.T, wide_z, precision=precise)
    raw = raw + lax.ppermute(raw, "c", swap)
    raw = from_all(raw, ("z", "y"), 16).sum(0)
    new_z = orth(raw.T)
    proj_z = jnp.dot(new_z, new_z.T, precision=precise)

    wide_v = jnp.einsum("vbz,zr->bvr", block, new_z, precision=precise)
    gram_v = jnp.einsum("bvr,bwr->vw", wide_v, wide_v, precision=precise)
    gram_v = from_all(gram_v.reshape(8, 128), ("z", "y", "c"), 32).sum(0).reshape(32, 32)
    new_v = orth(jnp.dot(gram_v, factor_v, precision=precise))
    proj_v = jnp.dot(new_v, new_v.T, precision=precise)
    total = jnp.sum(new_v * jnp.dot(gram_v, new_v, precision=precise))
    core_rms = jnp.sqrt(total / (16 * 16 * 64 * 64))
    return (proj_z, proj_v, core_rms)


def solution(mesh):
    fine = Mesh(mesh.devices.reshape(4, 4, 2, 4), ("z", "y", "c", "x"))
    rows = ("z", "y", "c")
    in_specs = (P("x", None, rows, None), P(), P(rows, None), P(), P())
    out_specs = (P(), P(), P())
    return jax.shard_map(
        per_device, mesh=fine, in_specs=in_specs, out_specs=out_specs, check_vma=False
    )
```

```python
import jax
import jax.numpy as jnp
from jax import lax
from jax.experimental import pallas as pl
from jax.experimental.pallas import tpu as pltpu
from jax.sharding import Mesh, PartitionSpec as P

precise = lax.Precision.HIGHEST
swap = [(0, 1), (1, 0)]


def from_all(value, axes, count):
    copies = jnp.broadcast_to(value[None], (count,) + value.shape)
    return lax.all_to_all(copies, axes, 0, 0, tiled=True)


def product(left, right, contract):
    return lax.dot_general(
        left, right, (contract, ((), ())), precision=precise,
        preferred_element_type=jnp.float32,
    )


def orth_rows(rows):
    count, width = rows.shape
    gram = product(rows, rows, ((1,), (1,)))
    tiles = count // 8
    left = [gram[8 * t:8 * t + 8, :] for t in range(tiles)]
    right = [rows[8 * t:8 * t + 8, :] for t in range(tiles)]
    sub_left = lax.broadcasted_iota(jnp.int32, (8, count), 0)
    sub_right = lax.broadcasted_iota(jnp.int32, (8, width), 0)
    done = []
    for p in range(tiles):
        cols = [
            {t: jnp.broadcast_to(left[t][:, 8 * p + j:8 * p + j + 1], (8, width)) for t in range(p, tiles)}
            for j in range(8)
        ]
        scale = jnp.zeros((8, width), jnp.float32)
        for k in range(8):
            pivot = cols[k][p][k:k + 1, :]
            inverse = 1.0 / pivot
            scale = jnp.where(sub_right == k, lax.rsqrt(pivot), scale)
            row_left = left[p][k:k + 1, :] * inverse[:, :count]
            row_right = right[p][k:k + 1, :] * inverse
            row_cols = [cols[j][p][k:k + 1, :] * inverse for j in range(8)]
            for t in range(p, tiles):
                factor = cols[k][t]
                if t == p:
                    factor = jnp.where(sub_right > k, factor, 0.0)
                left[t] = left[t] - factor[:, :count] * row_left
                right[t] = right[t] - factor * row_right
                for j in range(k + 1, 8):
                    cols[j][t] = cols[j][t] - factor * row_cols[j]
        done.append(right[p] * scale)
    return jnp.concatenate(done, axis=0)


def z_kernel(raws_ref, block_ref, proj_ref, grams_ref):
    raw = raws_ref[0]
    for i in range(1, 16):
        raw = raw + raws_ref[i]
    basis = orth_rows(raw)
    proj_ref[...] = product(basis, basis, ((0,), (0,)))
    none = jnp.zeros((64, 128), jnp.float32)
    pair = jnp.concatenate(
        [jnp.concatenate([basis, none], axis=1), jnp.concatenate([none, basis], axis=1)], axis=0
    )
    block = block_ref[...].reshape(4, 16, 2, 8, 128)
    gram = jnp.zeros((32, 32), jnp.float32)
    joined = jnp.concatenate(
        [
            jnp.concatenate([block[:, b, 0].reshape(32, 128), block[:, b, 1].reshape(32, 128)], axis=1)
            for b in range(16)
        ],
        axis=0,
    )
    wide = product(joined, pair, ((1,), (1,)))
    flat = jnp.concatenate([wide[32 * b:32 * b + 32] for b in range(16)], axis=1)
    gram = product(flat, flat, ((1,), (1,)))
    packed = jnp.concatenate([gram[8 * i:8 * i + 8] for i in range(4)], axis=1)
    for i in range(32):
        grams_ref[i] = packed


def v_kernel(grams_ref, factor_ref, proj_ref, rms_ref):
    total = grams_ref[0]
    for i in range(1, 32):
        total = total + grams_ref[i]
    gram = jnp.concatenate([total[:, 32 * i:32 * i + 32] for i in range(4)], axis=0)
    raw = product(factor_ref[...], gram, ((0,), (1,)))
    basis = orth_rows(raw)
    proj_ref[...] = product(basis, basis, ((0,), (0,)))
    energy = jnp.sum(basis * product(basis, gram, ((1,), (0,))), axis=(0, 1), keepdims=True)
    rms_ref[...] = jnp.sqrt(energy / (16 * 16 * 64 * 64))


def per_device(field, factor_x, factor_y, factor_z, factor_v):
    core = lax.axis_index("c")
    other_y = lax.ppermute(factor_y, "c", swap)
    along_x = jnp.einsum("vxyz,xa->avyz", field, factor_x, precision=precise)
    keep = lax.dynamic_slice_in_dim(along_x, core * 8, 8, 0)
    send = lax.dynamic_slice_in_dim(along_x, (1 - core) * 8, 8, 0)
    got = lax.ppermute(send, "c", swap)
    both = jnp.concatenate([keep, got], axis=2)
    both_y = jnp.concatenate([factor_y, other_y], axis=0)
    part = jnp.einsum("avyz,yb->avbz", both, both_y, precision=precise)
    part = part.reshape(8, 8, 2, 32, 128).transpose(0, 2, 3, 1, 4).reshape(16, 32, 8, 128)
    parts = lax.all_to_all(part, ("z", "y"), 0, 0, tiled=True)
    block = from_all(parts.sum(0), "x", 4)

    wide_z = jnp.einsum("xbvz,xvc->bcz", block, factor_v.reshape(4, 8, 16), precision=precise).reshape(512, 128)
    small_core = jnp.dot(wide_z, factor_z, precision=precise)
    raw = jnp.dot(small_core.T, wide_z, precision=precise)
    raw = raw + lax.ppermute(raw, "c", swap)
    raws = from_all(raw, ("z", "y"), 16)
    proj_z, grams = pl.pallas_call(
        z_kernel,
        out_shape=(
            jax.ShapeDtypeStruct((128, 128), jnp.float32),
            jax.ShapeDtypeStruct((32, 8, 128), jnp.float32),
        ),
    )(raws, block)
    grams = lax.all_to_all(grams, ("z", "y", "c"), 0, 0, tiled=True)
    proj_v, core_rms = pl.pallas_call(
        v_kernel,
        out_shape=(
            jax.ShapeDtypeStruct((32, 32), jnp.float32),
            jax.ShapeDtypeStruct((1, 1), jnp.float32),
        ),
    )(grams, factor_v)
    return (proj_z, proj_v, core_rms[0, 0])


def solution(mesh):
    fine = Mesh(mesh.devices.reshape(4, 4, 2, 4), ("z", "y", "c", "x"))
    rows = ("z", "y", "c")
    in_specs = (P("x", None, rows, None), P(), P(rows, None), P(), P())
    out_specs = (P(), P(), P())
    return jax.shard_map(
        per_device, mesh=fine, in_specs=in_specs, out_specs=out_specs, check_vma=False
    )
```

```python
import jax
import jax.numpy as jnp
from jax import lax
from jax.experimental import pallas as pl
from jax.experimental.pallas import tpu as pltpu
from jax.sharding import Mesh, PartitionSpec as P

precise = lax.Precision.HIGHEST
swap = [(0, 1), (1, 0)]


def from_all(value, axes, count):
    copies = jnp.broadcast_to(value[None], (count,) + value.shape)
    return lax.all_to_all(copies, axes, 0, 0, tiled=True)


def product(left, right, contract):
    return lax.dot_general(
        left, right, (contract, ((), ())), precision=precise,
        preferred_element_type=jnp.float32,
    )


def halves(value):
    high = value.astype(jnp.bfloat16)
    low = (value - high.astype(jnp.float32)).astype(jnp.bfloat16)
    return high, low


def dot16(left, right):
    return lax.dot_general(
        left, right, (((1,), (0,)), ((), ())), preferred_element_type=jnp.float32
    )


def spread(factor, turn):
    pick = lax.broadcasted_iota(jnp.int32, (128, 16), 0) // 8 + turn
    pick = jnp.where(pick >= 16, pick - 16, pick)
    pick = (pick == lax.broadcasted_iota(jnp.int32, (128, 16), 1)).astype(jnp.float32)
    wide = lax.broadcasted_iota(jnp.int32, (32, 256), 1) // 8
    wide = (wide == lax.broadcasted_iota(jnp.int32, (32, 256), 0)).astype(jnp.float32)
    full = product(product(pick, factor, ((1,), (0,))), wide, ((1,), (0,)))
    row = lax.broadcasted_iota(jnp.int32, (128, 256), 0)
    col = lax.broadcasted_iota(jnp.int32, (128, 256), 1)
    return jnp.where((row & 7) == (col & 7), full, 0.0)


def x_kernel(core_ref, factor_ref, factor_y_ref, field_ref, keep_ref, send_ref, both_ref):
    step = pl.program_id(0)

    @pl.when(step == 0)
    def _():
        high, low = halves(spread(factor_ref[...], core_ref[0] * 8))
        both_ref[0:128, :] = high
        both_ref[128:256, :] = low
        send_ref[64, :, 0:64] = factor_y_ref[...]
        send_ref[64, :, 64:128] = factor_y_ref[...]

    count = field_ref.shape[0]
    for v in range(count):
        tile = jnp.concatenate(
            [field_ref[v, :, 8 * t:8 * t + 8, :].reshape(256, 128) for t in range(4)], axis=1
        )
        high, low = halves(tile)
        first = dot16(both_ref[...], high)
        total = first[:128] + (first[128:] + dot16(both_ref[0:128, :], low))
        for t in range(4):
            cut = total[:, 128 * t:128 * t + 128].reshape(16, 8, 128)
            keep_ref[:, step * count + v, 8 * t:8 * t + 8, :] = cut[:8]
            for a in range(8):
                send_ref[8 * a + step * count + v, 8 * t:8 * t + 8, :] = cut[8 + a]


def y_kernel(mine_ref, keep_ref, got_ref, part_ref):
    high, low = halves(jnp.concatenate([mine_ref[...], got_ref[64, :, 0:64]], axis=0).T)
    left = jnp.concatenate([high, low, high], axis=1)
    for a in range(8):
        tile = jnp.concatenate(
            [jnp.concatenate([keep_ref[a, v], got_ref[8 * a + v]], axis=0) for v in range(8)], axis=1
        )
        high, low = halves(tile)
        total = dot16(left, jnp.concatenate([high, high, low], axis=0))
        for v in range(8):
            cut = total[:, 128 * v:128 * v + 128]
            part_ref[2 * a, v] = cut[:32]
            part_ref[2 * a + 1, v] = cut[32:]


def raw_kernel(block_ref, factor_v_ref, factor_z_ref, raw_ref):
    left = spread(factor_v_ref[...], 0)
    tile = jnp.concatenate(
        [block_ref[:, :, 8 * t:8 * t + 8, :].reshape(256, 128) for t in range(4)], axis=1
    )
    wide = product(left, tile, ((1,), (0,)))
    wide = jnp.concatenate([wide[:, 128 * t:128 * t + 128] for t in range(4)], axis=0)
    small = product(wide, factor_z_ref[...], ((1,), (1,)))
    raw_ref[...] = product(small, wide, ((0,), (0,)))


def orth_rows(rows):
    count, width = rows.shape
    gram = product(rows, rows, ((1,), (1,)))
    tiles = count // 8
    left = [gram[8 * t:8 * t + 8, :] for t in range(tiles)]
    right = [rows[8 * t:8 * t + 8, :] for t in range(tiles)]
    sub_left = lax.broadcasted_iota(jnp.int32, (8, count), 0)
    sub_right = lax.broadcasted_iota(jnp.int32, (8, width), 0)
    done = []
    for p in range(tiles):
        cols = [
            {t: jnp.broadcast_to(left[t][:, 8 * p + j:8 * p + j + 1], (8, width)) for t in range(p, tiles)}
            for j in range(8)
        ]
        scale = jnp.zeros((8, width), jnp.float32)
        for k in range(8):
            pivot = cols[k][p][k:k + 1, :]
            inverse = 1.0 / pivot
            scale = jnp.where(sub_right == k, lax.rsqrt(pivot), scale)
            row_left = left[p][k:k + 1, :] * inverse[:, :count]
            row_right = right[p][k:k + 1, :] * inverse
            row_cols = [cols[j][p][k:k + 1, :] * inverse for j in range(8)]
            for t in range(p, tiles):
                factor = cols[k][t]
                if t == p:
                    factor = jnp.where(sub_right > k, factor, 0.0)
                left[t] = left[t] - factor[:, :count] * row_left
                right[t] = right[t] - factor * row_right
                for j in range(k + 1, 8):
                    cols[j][t] = cols[j][t] - factor * row_cols[j]
        done.append(right[p] * scale)
    return jnp.concatenate(done, axis=0)


def z_kernel(raws_ref, block_ref, proj_ref, grams_ref):
    raw = raws_ref[0]
    for i in range(1, 16):
        raw = raw + raws_ref[i]
    basis = orth_rows(raw)
    proj_ref[...] = product(basis, basis, ((0,), (0,)))
    none = jnp.zeros((64, 128), jnp.float32)
    pair = jnp.concatenate(
        [jnp.concatenate([basis, none], axis=1), jnp.concatenate([none, basis], axis=1)], axis=0
    )
    tiles = [block_ref[:, :, 8 * t:8 * t + 8, :].reshape(256, 128) for t in range(4)]
    wide = jnp.concatenate(
        [product(jnp.concatenate(tiles[t:t + 2], axis=1), pair, ((1,), (1,))) for t in (0, 2)], axis=1
    )
    outer = product(wide, wide, ((1,), (1,)))
    row = lax.broadcasted_iota(jnp.int32, (256, 256), 0)
    col = lax.broadcasted_iota(jnp.int32, (256, 256), 1)
    outer = jnp.where((row & 7) == (col & 7), outer, 0.0).reshape(32, 8, 256).sum(axis=1)
    fold = lax.broadcasted_iota(jnp.int32, (256, 32), 0) // 8
    fold = (fold == lax.broadcasted_iota(jnp.int32, (256, 32), 1)).astype(jnp.float32)
    gram = product(outer, fold, ((1,), (0,)))
    packed = jnp.concatenate([gram[8 * i:8 * i + 8] for i in range(4)], axis=1)
    for i in range(32):
        grams_ref[i] = packed


def v_kernel(grams_ref, factor_ref, proj_ref, rms_ref):
    total = grams_ref[0]
    for i in range(1, 32):
        total = total + grams_ref[i]
    gram = jnp.concatenate([total[:, 32 * i:32 * i + 32] for i in range(4)], axis=0)
    raw = product(factor_ref[...], gram, ((1,), (0,)))
    basis = orth_rows(raw)
    proj_ref[...] = product(basis, basis, ((0,), (0,)))
    energy = jnp.sum(basis * product(basis, gram, ((1,), (0,))), axis=(0, 1), keepdims=True)
    rms_ref[...] = jnp.sqrt(energy / (16 * 16 * 64 * 64))


def in_vmem(*shape):
    return pltpu.VMEM(shape, jnp.float32)


def fast(value):
    return pltpu.with_memory_space_constraint(value, pltpu.VMEM)


def slow(value):
    return pltpu.with_memory_space_constraint(value, pltpu.HBM)


def room(mib):
    return pltpu.CompilerParams(vmem_limit_bytes=mib << 20)


def whole():
    return pl.BlockSpec(memory_space=pltpu.VMEM)


def per_device(field, factor_x, factor_y, factor_z, factor_v):
    core = lax.axis_index("c").astype(jnp.int32).reshape(1)
    step = 2
    keep, send = pl.pallas_call(
        x_kernel,
        grid=(8 // step,),
        in_specs=[
            pl.BlockSpec(memory_space=pltpu.SMEM),
            whole(),
            whole(),
            pl.BlockSpec((step, 32, 32, 128), lambda i: (i, 0, 0, 0)),
        ],
        out_specs=(whole(), whole()),
        out_shape=(in_vmem(8, 8, 32, 128), in_vmem(65, 32, 128)),
        scratch_shapes=[pltpu.VMEM((256, 256), jnp.bfloat16)],
        compiler_params=room(12),
    )(core, slow(factor_x.T), slow(factor_y), slow(field))
    got = lax.ppermute(send, "c", swap)
    part = pl.pallas_call(
        y_kernel,
        in_specs=[whole()] * 3,
        out_specs=whole(),
        out_shape=in_vmem(16, 8, 32, 128),
        compiler_params=room(12),
    )(factor_y, fast(keep), fast(got))
    parts = lax.all_to_all(part, ("z", "y"), 0, 0, tiled=True)
    block = from_all(parts.sum(0), "x", 4)

    raw = pl.pallas_call(
        raw_kernel,
        in_specs=[whole()] * 3,
        out_specs=whole(),
        out_shape=in_vmem(64, 128),
        compiler_params=room(12),
    )(fast(block), factor_v.T, factor_z.T)
    raw = raw + lax.ppermute(raw, "c", swap)
    raws = from_all(raw, ("z", "y"), 16)
    proj_z, grams = pl.pallas_call(
        z_kernel,
        in_specs=[whole()] * 2,
        out_specs=(whole(), whole()),
        out_shape=(jax.ShapeDtypeStruct((128, 128), jnp.float32), in_vmem(32, 8, 128)),
        compiler_params=room(12),
    )(fast(raws), fast(block))
    grams = lax.all_to_all(grams, ("z", "y", "c"), 0, 0, tiled=True)
    proj_v, core_rms = pl.pallas_call(
        v_kernel,
        in_specs=[whole()] * 2,
        out_specs=(whole(), whole()),
        out_shape=(
            jax.ShapeDtypeStruct((32, 32), jnp.float32),
            jax.ShapeDtypeStruct((1, 1), jnp.float32),
        ),
        compiler_params=room(12),
    )(fast(grams), factor_v.T)
    return (proj_z, proj_v, core_rms[0, 0])


def solution(mesh):
    fine = Mesh(mesh.devices.reshape(4, 4, 2, 4), ("z", "y", "c", "x"))
    rows = ("z", "y", "c")
    in_specs = (P("x", None, rows, None), P(), P(rows, None), P(), P())
    out_specs = (P(), P(), P())
    return jax.shard_map(
        per_device, mesh=fine, in_specs=in_specs, out_specs=out_specs, check_vma=False
    )
```

```python
import jax
import jax.numpy as jnp
from jax import lax
from jax.experimental import pallas as pl
from jax.experimental.pallas import tpu as pltpu
from jax.sharding import Mesh, PartitionSpec as P

precise = lax.Precision.HIGHEST
swap = [(0, 1), (1, 0)]


def from_all(value, axes, count):
    copies = jnp.broadcast_to(value[None], (count,) + value.shape)
    return lax.all_to_all(copies, axes, 0, 0, tiled=True)


def gather_sum(slots, axis):
    got = [lax.ppermute(slots[k], axis, [(i, (i + k) % 4) for i in range(4)]) for k in (1, 3, 2)]
    return (slots[0] + got[0]) + (got[1] + got[2])


def product(left, right, contract):
    return lax.dot_general(
        left, right, (contract, ((), ())), precision=precise,
        preferred_element_type=jnp.float32,
    )


def halves(value):
    high = value.astype(jnp.bfloat16)
    low = (value - high.astype(jnp.float32)).astype(jnp.bfloat16)
    return high, low


def dot16(left, right):
    return lax.dot_general(
        left, right, (((1,), (0,)), ((), ())), preferred_element_type=jnp.float32
    )


def spread(factor, turn):
    pick = lax.broadcasted_iota(jnp.int32, (128, 16), 0) // 8 + turn
    pick = jnp.where(pick >= 16, pick - 16, pick)
    pick = (pick == lax.broadcasted_iota(jnp.int32, (128, 16), 1)).astype(jnp.float32)
    wide = lax.broadcasted_iota(jnp.int32, (32, 256), 1) // 8
    wide = (wide == lax.broadcasted_iota(jnp.int32, (32, 256), 0)).astype(jnp.float32)
    full = product(product(pick, factor, ((1,), (0,))), wide, ((1,), (0,)))
    row = lax.broadcasted_iota(jnp.int32, (128, 256), 0)
    col = lax.broadcasted_iota(jnp.int32, (128, 256), 1)
    return jnp.where((row & 7) == (col & 7), full, 0.0)


def x_kernel(core_ref, factor_ref, factor_y_ref, field_ref, keep_ref, send_ref, both_ref):
    step = pl.program_id(0)

    @pl.when(step == 0)
    def _():
        high, low = halves(spread(factor_ref[...], core_ref[0] * 8))
        both_ref[0:128, :] = high
        both_ref[128:256, :] = low
        send_ref[64, :, 0:64] = factor_y_ref[...]
        send_ref[64, :, 64:128] = factor_y_ref[...]

    count = field_ref.shape[0]
    for v in range(count):
        tile = jnp.concatenate(
            [field_ref[v, :, 8 * t:8 * t + 8, :].reshape(256, 128) for t in range(4)], axis=1
        )
        high, low = halves(tile)
        first = dot16(both_ref[...], high)
        total = first[:128] + (first[128:] + dot16(both_ref[0:128, :], low))
        for t in range(4):
            cut = total[:, 128 * t:128 * t + 128].reshape(16, 8, 128)
            keep_ref[:, step * count + v, 8 * t:8 * t + 8, :] = cut[:8]
            for a in range(8):
                send_ref[8 * a + step * count + v, 8 * t:8 * t + 8, :] = cut[8 + a]


def y_kernel(mine_ref, keep_ref, got_ref, y_first_ref, z_first_ref):
    my_y, my_z = lax.axis_index("y"), lax.axis_index("z")
    high, low = halves(jnp.concatenate([mine_ref[...], got_ref[64, :, 0:64]], axis=0).T)
    left = jnp.concatenate([high, low, high], axis=1)
    for a in range(8):
        tile = jnp.concatenate(
            [jnp.concatenate([keep_ref[a, v], got_ref[8 * a + v]], axis=0) for v in range(8)], axis=1
        )
        high, low = halves(tile)
        total = dot16(left, jnp.concatenate([high, high, low], axis=0))
        for half in range(2):
            to_z, to_y = divmod(2 * a + half, 4)
            dz, dy = (to_z - my_z + 4) % 4, (to_y - my_y + 4) % 4
            for v in range(4):
                y_first_ref[dy, dz, v] = total[32 * half:32 * half + 32, 128 * v:128 * v + 128]
                z_first_ref[dz, dy, v] = total[32 * half:32 * half + 32, 128 * v + 512:128 * v + 640]


def raw_kernel(block_ref, factor_v_ref, factor_z_ref, raw_ref):
    left = spread(factor_v_ref[...], 0)
    tile = jnp.concatenate(
        [block_ref[:, :, 8 * t:8 * t + 8, :].reshape(256, 128) for t in range(4)], axis=1
    )
    wide = product(left, tile, ((1,), (0,)))
    wide = jnp.concatenate([wide[:, 128 * t:128 * t + 128] for t in range(4)], axis=0)
    small = product(wide, factor_z_ref[...], ((1,), (1,)))
    raw_ref[...] = product(small, wide, ((0,), (0,)))


def orth_rows(rows):
    count, width = rows.shape
    gram = product(rows, rows, ((1,), (1,)))
    tiles = count // 8
    left = [gram[8 * t:8 * t + 8, :] for t in range(tiles)]
    right = [rows[8 * t:8 * t + 8, :] for t in range(tiles)]
    sub_left = lax.broadcasted_iota(jnp.int32, (8, count), 0)
    sub_right = lax.broadcasted_iota(jnp.int32, (8, width), 0)
    done = []
    for p in range(tiles):
        cols = [
            {t: jnp.broadcast_to(left[t][:, 8 * p + j:8 * p + j + 1], (8, width)) for t in range(p, tiles)}
            for j in range(8)
        ]
        scale = jnp.zeros((8, width), jnp.float32)
        for k in range(8):
            pivot = cols[k][p][k:k + 1, :]
            inverse = 1.0 / pivot
            scale = jnp.where(sub_right == k, lax.rsqrt(pivot), scale)
            row_left = left[p][k:k + 1, :] * inverse[:, :count]
            row_right = right[p][k:k + 1, :] * inverse
            row_cols = [cols[j][p][k:k + 1, :] * inverse for j in range(8)]
            for t in range(p, tiles):
                factor = cols[k][t]
                if t == p:
                    factor = jnp.where(sub_right > k, factor, 0.0)
                left[t] = left[t] - factor[:, :count] * row_left
                right[t] = right[t] - factor * row_right
                for j in range(k + 1, 8):
                    cols[j][t] = cols[j][t] - factor * row_cols[j]
        done.append(right[p] * scale)
    return jnp.concatenate(done, axis=0)


def z_kernel(raws_ref, block_ref, proj_ref, grams_ref):
    raw = raws_ref[0]
    for i in range(1, 16):
        raw = raw + raws_ref[i]
    basis = orth_rows(raw)
    proj_ref[...] = product(basis, basis, ((0,), (0,)))
    none = jnp.zeros((64, 128), jnp.float32)
    pair = jnp.concatenate(
        [jnp.concatenate([basis, none], axis=1), jnp.concatenate([none, basis], axis=1)], axis=0
    )
    tiles = [block_ref[:, :, 8 * t:8 * t + 8, :].reshape(256, 128) for t in range(4)]
    wide = jnp.concatenate(
        [product(jnp.concatenate(tiles[t:t + 2], axis=1), pair, ((1,), (1,))) for t in (0, 2)], axis=1
    )
    outer = product(wide, wide, ((1,), (1,)))
    row = lax.broadcasted_iota(jnp.int32, (256, 256), 0)
    col = lax.broadcasted_iota(jnp.int32, (256, 256), 1)
    outer = jnp.where((row & 7) == (col & 7), outer, 0.0).reshape(32, 8, 256).sum(axis=1)
    fold = lax.broadcasted_iota(jnp.int32, (256, 32), 0) // 8
    fold = (fold == lax.broadcasted_iota(jnp.int32, (256, 32), 1)).astype(jnp.float32)
    gram = product(outer, fold, ((1,), (0,)))
    packed = jnp.concatenate([gram[8 * i:8 * i + 8] for i in range(4)], axis=1)
    for i in range(32):
        grams_ref[i] = packed


def v_kernel(grams_ref, factor_ref, proj_ref, rms_ref):
    total = grams_ref[0]
    for i in range(1, 32):
        total = total + grams_ref[i]
    gram = jnp.concatenate([total[:, 32 * i:32 * i + 32] for i in range(4)], axis=0)
    raw = product(factor_ref[...], gram, ((1,), (0,)))
    basis = orth_rows(raw)
    proj_ref[...] = product(basis, basis, ((0,), (0,)))
    energy = jnp.sum(basis * product(basis, gram, ((1,), (0,))), axis=(0, 1), keepdims=True)
    rms_ref[...] = jnp.sqrt(energy / (16 * 16 * 64 * 64))


def in_vmem(*shape):
    return pltpu.VMEM(shape, jnp.float32)


def fast(value):
    return pltpu.with_memory_space_constraint(value, pltpu.VMEM)


def slow(value):
    return pltpu.with_memory_space_constraint(value, pltpu.HBM)


def room(mib):
    return pltpu.CompilerParams(vmem_limit_bytes=mib << 20)


def whole():
    return pl.BlockSpec(memory_space=pltpu.VMEM)


def per_device(field, factor_x, factor_y, factor_z, factor_v):
    core = lax.axis_index("c").astype(jnp.int32).reshape(1)
    step = 2
    keep, send = pl.pallas_call(
        x_kernel,
        grid=(8 // step,),
        in_specs=[
            pl.BlockSpec(memory_space=pltpu.SMEM),
            whole(),
            whole(),
            pl.BlockSpec((step, 32, 32, 128), lambda i: (i, 0, 0, 0)),
        ],
        out_specs=(whole(), whole()),
        out_shape=(in_vmem(8, 8, 32, 128), in_vmem(65, 32, 128)),
        scratch_shapes=[pltpu.VMEM((256, 256), jnp.bfloat16)],
        compiler_params=room(12),
    )(core, slow(factor_x.T), slow(factor_y), slow(field))
    got = lax.ppermute(send, "c", swap)
    y_first, z_first = pl.pallas_call(
        y_kernel,
        in_specs=[whole()] * 3,
        out_specs=(whole(), whole()),
        out_shape=(in_vmem(4, 4, 4, 32, 128), in_vmem(4, 4, 4, 32, 128)),
        compiler_params=room(12),
    )(factor_y, fast(keep), fast(got))
    y_done, z_done = gather_sum(y_first, "y"), gather_sum(z_first, "z")
    block = jnp.concatenate([gather_sum(y_done, "z"), gather_sum(z_done, "y")], axis=0)
    block = from_all(block, "x", 4)

    raw = pl.pallas_call(
        raw_kernel,
        in_specs=[whole()] * 3,
        out_specs=whole(),
        out_shape=in_vmem(64, 128),
        compiler_params=room(12),
    )(fast(block), factor_v.T, factor_z.T)
    raw = raw + lax.ppermute(raw, "c", swap)
    raws = from_all(raw, ("z", "y"), 16)
    proj_z, grams = pl.pallas_call(
        z_kernel,
        in_specs=[whole()] * 2,
        out_specs=(whole(), whole()),
        out_shape=(jax.ShapeDtypeStruct((128, 128), jnp.float32), in_vmem(32, 8, 128)),
        compiler_params=room(12),
    )(fast(raws), fast(block))
    grams = lax.all_to_all(grams, ("z", "y", "c"), 0, 0, tiled=True)
    proj_v, core_rms = pl.pallas_call(
        v_kernel,
        in_specs=[whole()] * 2,
        out_specs=(whole(), whole()),
        out_shape=(
            jax.ShapeDtypeStruct((32, 32), jnp.float32),
            jax.ShapeDtypeStruct((1, 1), jnp.float32),
        ),
        compiler_params=room(12),
    )(fast(grams), factor_v.T)
    return (proj_z, proj_v, core_rms[0, 0])


def solution(mesh):
    fine = Mesh(mesh.devices.reshape(4, 4, 2, 4), ("z", "y", "c", "x"))
    rows = ("z", "y", "c")
    in_specs = (P("x", None, rows, None), P(), P(rows, None), P(), P())
    out_specs = (P(), P(), P())
    return jax.shard_map(
        per_device, mesh=fine, in_specs=in_specs, out_specs=out_specs, check_vma=False
    )
```

```python
import jax
import jax.numpy as jnp
from jax import lax
from jax.experimental import pallas as pl
from jax.experimental.pallas import tpu as pltpu
from jax.sharding import Mesh, PartitionSpec as P

precise = lax.Precision.HIGHEST
swap = [(0, 1), (1, 0)]


def from_all(value, axes, count):
    copies = jnp.broadcast_to(value[None], (count,) + value.shape)
    return lax.all_to_all(copies, axes, 0, 0, tiled=True)


def hops(step, first):
    pairs = []
    for z in range(4):
        for y in range(4):
            for c in range(2):
                along_y = (c == 0) == first
                to_z, to_y = (z, (y + step) % 4) if along_y else ((z + step) % 4, y)
                pairs.append((8 * z + 2 * y + c, 8 * to_z + 2 * to_y + c))
    return pairs


def gather_sum(slots, first):
    got = [lax.ppermute(slots[k], ("z", "y", "c"), hops(k, first)) for k in (2, 1, 3)]
    return (slots[0] + got[0]) + (got[1] + got[2])


def product(left, right, contract):
    return lax.dot_general(
        left, right, (contract, ((), ())), precision=precise,
        preferred_element_type=jnp.float32,
    )


def halves(value):
    high = value.astype(jnp.bfloat16)
    low = (value - high.astype(jnp.float32)).astype(jnp.bfloat16)
    return high, low


def dot16(left, right):
    return lax.dot_general(
        left, right, (((1,), (0,)), ((), ())), preferred_element_type=jnp.float32
    )


def spread(factor, turn):
    pick = lax.broadcasted_iota(jnp.int32, (128, 16), 0) // 8 + turn
    pick = jnp.where(pick >= 16, pick - 16, pick)
    pick = (pick == lax.broadcasted_iota(jnp.int32, (128, 16), 1)).astype(jnp.float32)
    wide = lax.broadcasted_iota(jnp.int32, (32, 256), 1) // 8
    wide = (wide == lax.broadcasted_iota(jnp.int32, (32, 256), 0)).astype(jnp.float32)
    full = product(product(pick, factor, ((1,), (0,))), wide, ((1,), (0,)))
    row = lax.broadcasted_iota(jnp.int32, (128, 256), 0)
    col = lax.broadcasted_iota(jnp.int32, (128, 256), 1)
    return jnp.where((row & 7) == (col & 7), full, 0.0)


def x_kernel(core_ref, factor_ref, factor_y_ref, field_ref, keep_ref, send_ref, both_ref):
    step = pl.program_id(0)

    @pl.when(step == 0)
    def _():
        high, low = halves(spread(factor_ref[...], core_ref[0] * 8))
        both_ref[0:128, :] = high
        both_ref[128:256, :] = low
        send_ref[64, :, 0:64] = factor_y_ref[...]
        send_ref[64, :, 64:128] = factor_y_ref[...]

    count = field_ref.shape[0]
    for v in range(count):
        tile = jnp.concatenate(
            [field_ref[v, :, 8 * t:8 * t + 8, :].reshape(256, 128) for t in range(4)], axis=1
        )
        high, low = halves(tile)
        first = dot16(both_ref[...], high)
        total = first[:128] + (first[128:] + dot16(both_ref[0:128, :], low))
        for t in range(4):
            cut = total[:, 128 * t:128 * t + 128].reshape(16, 8, 128)
            keep_ref[:, step * count + v, 8 * t:8 * t + 8, :] = cut[:8]
            for a in range(8):
                send_ref[8 * a + step * count + v, 8 * t:8 * t + 8, :] = cut[8 + a]


def y_kernel(mine_ref, keep_ref, got_ref, slots_ref):
    my_y, my_z, core = lax.axis_index("y"), lax.axis_index("z"), lax.axis_index("c")
    high, low = halves(jnp.concatenate([mine_ref[...], got_ref[64, :, 0:64]], axis=0).T)
    left = jnp.concatenate([high, low, high], axis=1)
    for a in range(8):
        tile = jnp.concatenate(
            [jnp.concatenate([keep_ref[a, v], got_ref[8 * a + v]], axis=0) for v in range(8)], axis=1
        )
        high, low = halves(tile)
        total = dot16(left, jnp.concatenate([high, high, low], axis=0))
        for half in range(2):
            to_z, to_y = divmod(2 * a + half, 4)
            dz, dy = (to_z - my_z + 4) % 4, (to_y - my_y + 4) % 4
            first = dy + core * (dz - dy)
            second = dz + core * (dy - dz)
            for v in range(8):
                slots_ref[first, second, v] = total[32 * half:32 * half + 32, 128 * v:128 * v + 128]


def spread_kernel(factor_ref, spread_ref):
    spread_ref[...] = spread(factor_ref[...], 0)


def raw_kernel(mine_ref, one_ref, two_ref, three_ref, spread_ref, factor_z_ref, raw_ref, block_ref):
    my_x = lax.axis_index("x")
    for back, ref in enumerate((mine_ref, one_ref, two_ref, three_ref)):
        block_ref[(my_x - back + 4) % 4] = ref[...]
    left = spread_ref[...]
    tile = jnp.concatenate(
        [block_ref[:, :, 8 * t:8 * t + 8, :].reshape(256, 128) for t in range(4)], axis=1
    )
    wide = product(left, tile, ((1,), (0,)))
    wide = jnp.concatenate([wide[:, 128 * t:128 * t + 128] for t in range(4)], axis=0)
    small = product(wide, factor_z_ref[...], ((1,), (1,)))
    raw_ref[...] = product(small, wide, ((0,), (0,)))


def orth_rows(rows):
    count, width = rows.shape
    gram = product(rows, rows, ((1,), (1,)))
    tiles = count // 8
    left = [gram[8 * t:8 * t + 8, :] for t in range(tiles)]
    right = [rows[8 * t:8 * t + 8, :] for t in range(tiles)]
    sub_left = lax.broadcasted_iota(jnp.int32, (8, count), 0)
    sub_right = lax.broadcasted_iota(jnp.int32, (8, width), 0)
    done = []
    for p in range(tiles):
        cols = [
            {t: jnp.broadcast_to(left[t][:, 8 * p + j:8 * p + j + 1], (8, width)) for t in range(p, tiles)}
            for j in range(8)
        ]
        scale = jnp.zeros((8, width), jnp.float32)
        for k in range(8):
            pivot = cols[k][p][k:k + 1, :]
            inverse = 1.0 / pivot
            scale = jnp.where(sub_right == k, lax.rsqrt(pivot), scale)
            row_left = left[p][k:k + 1, :] * inverse[:, :count]
            row_right = right[p][k:k + 1, :] * inverse
            row_cols = [cols[j][p][k:k + 1, :] * inverse for j in range(8)]
            for t in range(p, tiles):
                factor = cols[k][t]
                if t == p:
                    factor = jnp.where(sub_right > k, factor, 0.0)
                left[t] = left[t] - factor[:, :count] * row_left
                right[t] = right[t] - factor * row_right
                for j in range(k + 1, 8):
                    cols[j][t] = cols[j][t] - factor * row_cols[j]
        done.append(right[p] * scale)
    return jnp.concatenate(done, axis=0)


def z_kernel(raws_ref, block_ref, proj_ref, grams_ref):
    raw = raws_ref[0]
    for i in range(1, 16):
        raw = raw + raws_ref[i]
    basis = orth_rows(raw)
    proj_ref[...] = product(basis, basis, ((0,), (0,)))
    none = jnp.zeros((64, 128), jnp.float32)
    pair = jnp.concatenate(
        [jnp.concatenate([basis, none], axis=1), jnp.concatenate([none, basis], axis=1)], axis=0
    )
    tiles = [block_ref[:, :, 8 * t:8 * t + 8, :].reshape(256, 128) for t in range(4)]
    wide = jnp.concatenate(
        [product(jnp.concatenate(tiles[t:t + 2], axis=1), pair, ((1,), (1,))) for t in (0, 2)], axis=1
    )
    outer = product(wide, wide, ((1,), (1,)))
    row = lax.broadcasted_iota(jnp.int32, (256, 256), 0)
    col = lax.broadcasted_iota(jnp.int32, (256, 256), 1)
    outer = jnp.where((row & 7) == (col & 7), outer, 0.0).reshape(32, 8, 256).sum(axis=1)
    fold = lax.broadcasted_iota(jnp.int32, (256, 32), 0) // 8
    fold = (fold == lax.broadcasted_iota(jnp.int32, (256, 32), 1)).astype(jnp.float32)
    gram = product(outer, fold, ((1,), (0,)))
    packed = jnp.concatenate([gram[8 * i:8 * i + 8] for i in range(4)], axis=1)
    for i in range(32):
        grams_ref[i] = packed


def v_kernel(grams_ref, factor_ref, proj_ref, rms_ref):
    total = grams_ref[0]
    for i in range(1, 32):
        total = total + grams_ref[i]
    gram = jnp.concatenate([total[:, 32 * i:32 * i + 32] for i in range(4)], axis=0)
    raw = product(factor_ref[...], gram, ((1,), (0,)))
    basis = orth_rows(raw)
    proj_ref[...] = product(basis, basis, ((0,), (0,)))
    energy = jnp.sum(basis * product(basis, gram, ((1,), (0,))), axis=(0, 1), keepdims=True)
    rms_ref[...] = jnp.sqrt(energy / (16 * 16 * 64 * 64))


def in_vmem(*shape):
    return pltpu.VMEM(shape, jnp.float32)


def fast(value):
    return pltpu.with_memory_space_constraint(value, pltpu.VMEM)


def slow(value):
    return pltpu.with_memory_space_constraint(value, pltpu.HBM)


def room(mib):
    return pltpu.CompilerParams(vmem_limit_bytes=mib << 20)


def whole():
    return pl.BlockSpec(memory_space=pltpu.VMEM)


def per_device(field, factor_x, factor_y, factor_z, factor_v):
    core = lax.axis_index("c").astype(jnp.int32).reshape(1)
    step = 2
    keep, send = pl.pallas_call(
        x_kernel,
        grid=(8 // step,),
        in_specs=[
            pl.BlockSpec(memory_space=pltpu.SMEM),
            whole(),
            whole(),
            pl.BlockSpec((step, 32, 32, 128), lambda i: (i, 0, 0, 0)),
        ],
        out_specs=(whole(), whole()),
        out_shape=(in_vmem(8, 8, 32, 128), in_vmem(65, 32, 128)),
        scratch_shapes=[pltpu.VMEM((256, 256), jnp.bfloat16)],
        compiler_params=room(12),
    )(core, slow(factor_x.T), slow(factor_y), slow(field))
    got = lax.ppermute(send, "c", swap)
    late_v, keep = lax.optimization_barrier((factor_v.T, keep))
    wide_v = pl.pallas_call(
        spread_kernel,
        in_specs=[whole()],
        out_specs=whole(),
        out_shape=in_vmem(128, 256),
        compiler_params=room(4),
    )(late_v)
    slots = pl.pallas_call(
        y_kernel,
        in_specs=[whole()] * 3,
        out_specs=whole(),
        out_shape=in_vmem(4, 4, 8, 32, 128),
        compiler_params=room(12),
    )(factor_y, fast(keep), fast(got))
    mine = gather_sum(gather_sum(slots, True), False)
    one, two, three = [
        lax.ppermute(mine, "x", [(i, (i + k) % 4) for i in range(4)]) for k in (1, 2, 3)
    ]
    raw, block = pl.pallas_call(
        raw_kernel,
        in_specs=[whole()] * 6,
        out_specs=(whole(), whole()),
        out_shape=(in_vmem(64, 128), in_vmem(4, 8, 32, 128)),
        compiler_params=room(12),
    )(fast(mine), fast(one), fast(two), fast(three), fast(wide_v), factor_z.T)
    raw = raw + lax.ppermute(raw, "c", swap)
    raws = from_all(raw, ("z", "y"), 16)
    proj_z, grams = pl.pallas_call(
        z_kernel,
        in_specs=[whole()] * 2,
        out_specs=(whole(), whole()),
        out_shape=(jax.ShapeDtypeStruct((128, 128), jnp.float32), in_vmem(32, 8, 128)),
        compiler_params=room(12),
    )(fast(raws), fast(block))
    grams = lax.all_to_all(grams, ("z", "y", "c"), 0, 0, tiled=True)
    proj_v, core_rms = pl.pallas_call(
        v_kernel,
        in_specs=[whole()] * 2,
        out_specs=(whole(), whole()),
        out_shape=(
            jax.ShapeDtypeStruct((32, 32), jnp.float32),
            jax.ShapeDtypeStruct((1, 1), jnp.float32),
        ),
        compiler_params=room(12),
    )(fast(grams), factor_v.T)
    return (proj_z, proj_v, core_rms[0, 0])


def solution(mesh):
    fine = Mesh(mesh.devices.reshape(4, 4, 2, 4), ("z", "y", "c", "x"))
    rows = ("z", "y", "c")
    in_specs = (P("x", None, rows, None), P(), P(rows, None), P(), P())
    out_specs = (P(), P(), P())
    return jax.shard_map(
        per_device, mesh=fine, in_specs=in_specs, out_specs=out_specs, check_vma=False
    )
```

```python
import jax
import jax.numpy as jnp
from jax import lax
from jax.experimental import pallas as pl
from jax.experimental.pallas import tpu as pltpu
from jax.sharding import Mesh, PartitionSpec as P

precise = lax.Precision.HIGHEST
swap = [(0, 1), (1, 0)]


def hops(step, first):
    pairs = []
    for z in range(4):
        for y in range(4):
            for c in range(2):
                along_y = (c == 0) == first
                to_z, to_y = (z, (y + step) % 4) if along_y else ((z + step) % 4, y)
                pairs.append((8 * z + 2 * y + c, 8 * to_z + 2 * to_y + c))
    return pairs


def gather_sum(slots, first):
    got = [lax.ppermute(slots[k], ("z", "y", "c"), hops(k, first)) for k in (2, 1, 3)]
    return (slots[0] + got[0]) + (got[1] + got[2])


def sum_all(value, axis):
    one, two, three = [
        lax.ppermute(value, axis, [(i, (i + k) % 4) for i in range(4)]) for k in (1, 2, 3)
    ]
    return (value + two) + (one + three)


def product(left, right, contract):
    return lax.dot_general(
        left, right, (contract, ((), ())), precision=precise,
        preferred_element_type=jnp.float32,
    )


def halves(value):
    high = value.astype(jnp.bfloat16)
    low = (value - high.astype(jnp.float32)).astype(jnp.bfloat16)
    return high, low


def product3(left, right, contract):
    (left_high, left_low), (right_high, right_low) = halves(left), halves(right)

    def one(a, b):
        return lax.dot_general(a, b, (contract, ((), ())), preferred_element_type=jnp.float32)

    return one(left_high, right_high) + (one(left_high, right_low) + one(left_low, right_high))


def dot16(left, right):
    return lax.dot_general(
        left, right, (((1,), (0,)), ((), ())), preferred_element_type=jnp.float32
    )


def spread(factor, turn):
    pick = lax.broadcasted_iota(jnp.int32, (128, 16), 0) // 8 + turn
    pick = jnp.where(pick >= 16, pick - 16, pick)
    pick = (pick == lax.broadcasted_iota(jnp.int32, (128, 16), 1)).astype(jnp.float32)
    wide = lax.broadcasted_iota(jnp.int32, (32, 256), 1) // 8
    wide = (wide == lax.broadcasted_iota(jnp.int32, (32, 256), 0)).astype(jnp.float32)
    full = product(product(pick, factor, ((1,), (0,))), wide, ((1,), (0,)))
    row = lax.broadcasted_iota(jnp.int32, (128, 256), 0)
    col = lax.broadcasted_iota(jnp.int32, (128, 256), 1)
    return jnp.where((row & 7) == (col & 7), full, 0.0)


def x_kernel(core_ref, factor_ref, factor_y_ref, field_ref, keep_ref, send_ref, both_ref):
    step = pl.program_id(0)

    @pl.when(step == 0)
    def _():
        high, low = halves(spread(factor_ref[...], core_ref[0] * 8))
        both_ref[0:128, :] = high
        both_ref[128:256, :] = low
        send_ref[64, :, 0:64] = factor_y_ref[...]
        send_ref[64, :, 64:128] = factor_y_ref[...]

    count = field_ref.shape[0]
    for v in range(count):
        tile = jnp.concatenate(
            [field_ref[v, :, 8 * t:8 * t + 8, :].reshape(256, 128) for t in range(4)], axis=1
        )
        high, low = halves(tile)
        first = dot16(both_ref[...], high)
        total = first[:128] + (first[128:] + dot16(both_ref[0:128, :], low))
        for t in range(4):
            cut = total[:, 128 * t:128 * t + 128].reshape(16, 8, 128)
            keep_ref[:, step * count + v, 8 * t:8 * t + 8, :] = cut[:8]
            for a in range(8):
                send_ref[8 * a + step * count + v, 8 * t:8 * t + 8, :] = cut[8 + a]


def y_kernel(mine_ref, keep_ref, got_ref, slots_ref):
    my_y, my_z, core = lax.axis_index("y"), lax.axis_index("z"), lax.axis_index("c")
    high, low = halves(jnp.concatenate([mine_ref[...], got_ref[64, :, 0:64]], axis=0).T)
    left = jnp.concatenate([high, low, high], axis=1)
    for a in range(8):
        tile = jnp.concatenate(
            [jnp.concatenate([keep_ref[a, v], got_ref[8 * a + v]], axis=0) for v in range(8)], axis=1
        )
        high, low = halves(tile)
        total = dot16(left, jnp.concatenate([high, high, low], axis=0))
        for half in range(2):
            to_z, to_y = divmod(2 * a + half, 4)
            dz, dy = (to_z - my_z + 4) % 4, (to_y - my_y + 4) % 4
            first = dy + core * (dz - dy)
            second = dz + core * (dy - dz)
            for v in range(8):
                slots_ref[first, second, v] = total[32 * half:32 * half + 32, 128 * v:128 * v + 128]


def spread_kernel(factor_ref, spread_ref):
    spread_ref[...] = spread(factor_ref[...], 0)


def raw_kernel(mine_ref, one_ref, two_ref, three_ref, spread_ref, factor_z_ref, raw_ref, block_ref):
    my_x = lax.axis_index("x")
    for back, ref in enumerate((mine_ref, one_ref, two_ref, three_ref)):
        block_ref[(my_x - back + 4) % 4] = ref[...]
    left = spread_ref[...]
    tile = jnp.concatenate(
        [block_ref[:, :, 8 * t:8 * t + 8, :].reshape(256, 128) for t in range(4)], axis=1
    )
    wide = product3(left, tile, ((1,), (0,)))
    wide = jnp.concatenate([wide[:, 128 * t:128 * t + 128] for t in range(4)], axis=0)
    small = product3(wide, factor_z_ref[...], ((1,), (1,)))
    raw_ref[...] = product3(small, wide, ((0,), (0,)))


def orth_rows(rows):
    count, width = rows.shape
    gram = product(rows, rows, ((1,), (1,)))
    tiles = count // 8
    left = [gram[8 * t:8 * t + 8, :] for t in range(tiles)]
    right = [rows[8 * t:8 * t + 8, :] for t in range(tiles)]
    sub_left = lax.broadcasted_iota(jnp.int32, (8, count), 0)
    sub_right = lax.broadcasted_iota(jnp.int32, (8, width), 0)
    done = []
    for p in range(tiles):
        cols = [
            {t: jnp.broadcast_to(left[t][:, 8 * p + j:8 * p + j + 1], (8, width)) for t in range(p, tiles)}
            for j in range(8)
        ]
        scale = jnp.zeros((8, width), jnp.float32)
        for k in range(8):
            pivot = cols[k][p][k:k + 1, :]
            inverse = 1.0 / pivot
            scale = jnp.where(sub_right == k, lax.rsqrt(pivot), scale)
            row_left = left[p][k:k + 1, :] * inverse[:, :count]
            row_right = right[p][k:k + 1, :] * inverse
            row_cols = [cols[j][p][k:k + 1, :] * inverse for j in range(8)]
            for t in range(p, tiles):
                factor = cols[k][t]
                if t == p:
                    factor = jnp.where(sub_right > k, factor, 0.0)
                left[t] = left[t] - factor[:, :count] * row_left
                right[t] = right[t] - factor * row_right
                for j in range(k + 1, 8):
                    cols[j][t] = cols[j][t] - factor * row_cols[j]
        done.append(right[p] * scale)
    return jnp.concatenate(done, axis=0)


def z_kernel(rows_ref, block_ref, proj_ref, grams_ref):
    basis = orth_rows(rows_ref[...])
    proj_ref[...] = product3(basis, basis, ((0,), (0,)))
    none = jnp.zeros((64, 128), jnp.float32)
    pair = jnp.concatenate(
        [jnp.concatenate([basis, none], axis=1), jnp.concatenate([none, basis], axis=1)], axis=0
    )
    tiles = [block_ref[:, :, 8 * t:8 * t + 8, :].reshape(256, 128) for t in range(4)]
    wide = jnp.concatenate(
        [product3(jnp.concatenate(tiles[t:t + 2], axis=1), pair, ((1,), (1,))) for t in (0, 2)], axis=1
    )
    outer = product3(wide, wide, ((1,), (1,)))
    row = lax.broadcasted_iota(jnp.int32, (256, 256), 0)
    col = lax.broadcasted_iota(jnp.int32, (256, 256), 1)
    outer = jnp.where((row & 7) == (col & 7), outer, 0.0).reshape(32, 8, 256).sum(axis=1)
    fold = lax.broadcasted_iota(jnp.int32, (256, 32), 0) // 8
    fold = (fold == lax.broadcasted_iota(jnp.int32, (256, 32), 1)).astype(jnp.float32)
    gram = product(outer, fold, ((1,), (0,)))
    packed = jnp.concatenate([gram[8 * i:8 * i + 8] for i in range(4)], axis=1)
    for i in range(32):
        grams_ref[i] = packed


def v_kernel(grams_ref, factor_ref, proj_ref, rms_ref):
    total = grams_ref[0]
    for i in range(1, 32):
        total = total + grams_ref[i]
    gram = jnp.concatenate([total[:, 32 * i:32 * i + 32] for i in range(4)], axis=0)
    raw = product(factor_ref[...], gram, ((1,), (0,)))
    basis = orth_rows(raw)
    proj_ref[...] = product3(basis, basis, ((0,), (0,)))
    energy = jnp.sum(basis * product3(basis, gram, ((1,), (0,))), axis=(0, 1), keepdims=True)
    rms_ref[...] = jnp.sqrt(energy / (16 * 16 * 64 * 64))


def in_vmem(*shape):
    return pltpu.VMEM(shape, jnp.float32)


def fast(value):
    return pltpu.with_memory_space_constraint(value, pltpu.VMEM)


def slow(value):
    return pltpu.with_memory_space_constraint(value, pltpu.HBM)


def room(mib):
    return pltpu.CompilerParams(vmem_limit_bytes=mib << 20)


def whole():
    return pl.BlockSpec(memory_space=pltpu.VMEM)


def per_device(field, factor_x, factor_y, factor_z, factor_v):
    core = lax.axis_index("c").astype(jnp.int32).reshape(1)
    step = 2
    keep, send = pl.pallas_call(
        x_kernel,
        grid=(8 // step,),
        in_specs=[
            pl.BlockSpec(memory_space=pltpu.SMEM),
            whole(),
            whole(),
            pl.BlockSpec((step, 32, 32, 128), lambda i: (i, 0, 0, 0)),
        ],
        out_specs=(whole(), whole()),
        out_shape=(in_vmem(8, 8, 32, 128), in_vmem(65, 32, 128)),
        scratch_shapes=[pltpu.VMEM((256, 256), jnp.bfloat16)],
        compiler_params=room(12),
    )(core, slow(factor_x.T), slow(factor_y), slow(field))
    got = lax.ppermute(send, "c", swap)
    late_v, keep = lax.optimization_barrier((factor_v.T, keep))
    wide_v = pl.pallas_call(
        spread_kernel,
        in_specs=[whole()],
        out_specs=whole(),
        out_shape=in_vmem(128, 256),
        compiler_params=room(4),
    )(late_v)
    slots = pl.pallas_call(
        y_kernel,
        in_specs=[whole()] * 3,
        out_specs=whole(),
        out_shape=in_vmem(4, 4, 8, 32, 128),
        compiler_params=room(12),
    )(factor_y, fast(keep), fast(got))
    mine = gather_sum(gather_sum(slots, True), False)
    one, two, three = [
        lax.ppermute(mine, "x", [(i, (i + k) % 4) for i in range(4)]) for k in (1, 2, 3)
    ]
    raw, block = pl.pallas_call(
        raw_kernel,
        in_specs=[whole()] * 6,
        out_specs=(whole(), whole()),
        out_shape=(in_vmem(64, 128), in_vmem(4, 8, 32, 128)),
        compiler_params=room(12),
    )(fast(mine), fast(one), fast(two), fast(three), fast(wide_v), factor_z.T)
    raw = raw + lax.ppermute(raw, "c", swap)
    raw = sum_all(sum_all(raw, "y"), "z")
    proj_z, grams = pl.pallas_call(
        z_kernel,
        in_specs=[whole()] * 2,
        out_specs=(whole(), whole()),
        out_shape=(jax.ShapeDtypeStruct((128, 128), jnp.float32), in_vmem(32, 8, 128)),
        compiler_params=room(12),
    )(fast(raw), fast(block))
    grams = lax.all_to_all(grams, ("z", "y", "c"), 0, 0, tiled=True)
    proj_v, core_rms = pl.pallas_call(
        v_kernel,
        in_specs=[whole()] * 2,
        out_specs=(whole(), whole()),
        out_shape=(
            jax.ShapeDtypeStruct((32, 32), jnp.float32),
            jax.ShapeDtypeStruct((1, 1), jnp.float32),
        ),
        compiler_params=room(12),
    )(fast(grams), factor_v.T)
    return (proj_z, proj_v, core_rms[0, 0])


def solution(mesh):
    fine = Mesh(mesh.devices.reshape(4, 4, 2, 4), ("z", "y", "c", "x"))
    rows = ("z", "y", "c")
    in_specs = (P("x", None, rows, None), P(), P(rows, None), P(), P())
    out_specs = (P(), P(), P())
    return jax.shard_map(
        per_device, mesh=fine, in_specs=in_specs, out_specs=out_specs, check_vma=False
    )
```

```python
import jax
import jax.numpy as jnp
from jax import lax
from jax.experimental import pallas as pl
from jax.experimental.pallas import tpu as pltpu
from jax.sharding import Mesh, PartitionSpec as P

precise = lax.Precision.HIGHEST
swap = [(0, 1), (1, 0)]


def hops(step, first):
    pairs = []
    for z in range(4):
        for y in range(4):
            for c in range(2):
                along_y = (c == 0) == first
                to_z, to_y = (z, (y + step) % 4) if along_y else ((z + step) % 4, y)
                pairs.append((8 * z + 2 * y + c, 8 * to_z + 2 * to_y + c))
    return pairs


def gather_sum(slots, first):
    got = [lax.ppermute(slots[k], ("z", "y", "c"), hops(k, first)) for k in (2, 1, 3)]
    return (slots[0] + got[0]) + (got[1] + got[2])


def sum_all(value, axis):
    one, two, three = [
        lax.ppermute(value, axis, [(i, (i + k) % 4) for i in range(4)]) for k in (1, 2, 3)
    ]
    return (value + two) + (one + three)


def product(left, right, contract):
    return lax.dot_general(
        left, right, (contract, ((), ())), precision=precise,
        preferred_element_type=jnp.float32,
    )


def halves(value):
    high = value.astype(jnp.bfloat16)
    low = (value - high.astype(jnp.float32)).astype(jnp.bfloat16)
    return high, low


def product3(left, right, contract):
    (left_high, left_low), (right_high, right_low) = halves(left), halves(right)

    def one(a, b):
        return lax.dot_general(a, b, (contract, ((), ())), preferred_element_type=jnp.float32)

    return one(left_high, right_high) + (one(left_high, right_low) + one(left_low, right_high))


def dot16(left, right):
    return lax.dot_general(
        left, right, (((1,), (0,)), ((), ())), preferred_element_type=jnp.float32
    )


def spread(factor, turn):
    pick = lax.broadcasted_iota(jnp.int32, (128, 16), 0) // 8 + turn
    pick = jnp.where(pick >= 16, pick - 16, pick)
    pick = (pick == lax.broadcasted_iota(jnp.int32, (128, 16), 1)).astype(jnp.float32)
    wide = lax.broadcasted_iota(jnp.int32, (32, 256), 1) // 8
    wide = (wide == lax.broadcasted_iota(jnp.int32, (32, 256), 0)).astype(jnp.float32)
    full = product(product(pick, factor, ((1,), (0,))), wide, ((1,), (0,)))
    row = lax.broadcasted_iota(jnp.int32, (128, 256), 0)
    col = lax.broadcasted_iota(jnp.int32, (128, 256), 1)
    return jnp.where((row & 7) == (col & 7), full, 0.0)


def x_kernel(factor_ref, factor_y_ref, field_ref, keep_ref, send_ref, held, held_x, held_y, arrived, small):
    copies = [
        pltpu.make_async_copy(field_ref.at[4 * i:4 * i + 4], held.at[4 * i:4 * i + 4], arrived.at[i])
        for i in range(2)
    ]
    copy_x = pltpu.make_async_copy(factor_ref, held_x, small.at[0])
    copy_y = pltpu.make_async_copy(factor_y_ref, held_y, small.at[1])
    for copy in [copy_x, copy_y] + copies:
        copy.start()
    copy_x.wait()
    factor_high, factor_low = halves(spread(held_x[...], lax.axis_index("c") * 8))
    both = jnp.concatenate([factor_high, factor_low], axis=0)
    copy_y.wait()
    send_ref[64, :, 0:64] = held_y[...]
    send_ref[64, :, 64:128] = held_y[...]
    for v in range(8):
        if v % 4 == 0:
            copies[v // 4].wait()
        tile = jnp.concatenate(
            [held[v, :, 8 * t:8 * t + 8, :].reshape(256, 128) for t in range(4)], axis=1
        )
        high, low = halves(tile)
        first = dot16(both, high)
        total = first[:128] + (first[128:] + dot16(factor_high, low))
        for t in range(4):
            cut = total[:, 128 * t:128 * t + 128].reshape(16, 8, 128)
            keep_ref[:, v, 8 * t:8 * t + 8, :] = cut[:8]
            for a in range(8):
                send_ref[8 * a + v, 8 * t:8 * t + 8, :] = cut[8 + a]


def y_kernel(mine_ref, keep_ref, got_ref, slots_ref):
    my_y, my_z, core = lax.axis_index("y"), lax.axis_index("z"), lax.axis_index("c")
    high, low = halves(jnp.concatenate([mine_ref[...], got_ref[64, :, 0:64]], axis=0).T)
    left = jnp.concatenate([high, low, high], axis=1)
    for a in range(8):
        tile = jnp.concatenate(
            [jnp.concatenate([keep_ref[a, v], got_ref[8 * a + v]], axis=0) for v in range(8)], axis=1
        )
        high, low = halves(tile)
        total = dot16(left, jnp.concatenate([high, high, low], axis=0))
        for half in range(2):
            to_z, to_y = divmod(2 * a + half, 4)
            dz, dy = (to_z - my_z + 4) % 4, (to_y - my_y + 4) % 4
            first = dy + core * (dz - dy)
            second = dz + core * (dy - dz)
            for v in range(8):
                slots_ref[first, second, v] = total[32 * half:32 * half + 32, 128 * v:128 * v + 128]


def spread_kernel(factor_ref, spread_ref):
    spread_ref[...] = spread(factor_ref[...], 0)


def raw_kernel(mine_ref, one_ref, two_ref, three_ref, spread_ref, factor_z_ref, raw_ref, block_ref):
    my_x = lax.axis_index("x")
    for back, ref in enumerate((mine_ref, one_ref, two_ref, three_ref)):
        block_ref[(my_x - back + 4) % 4] = ref[...]
    left = spread_ref[...]
    tile = jnp.concatenate(
        [block_ref[:, :, 8 * t:8 * t + 8, :].reshape(256, 128) for t in range(4)], axis=1
    )
    wide = product3(left, tile, ((1,), (0,)))
    wide = jnp.concatenate([wide[:, 128 * t:128 * t + 128] for t in range(4)], axis=0)
    small = product3(wide, factor_z_ref[...], ((1,), (1,)))
    raw_ref[...] = product3(small, wide, ((0,), (0,)))


def orth_rows(rows):
    count, width = rows.shape
    gram = product(rows, rows, ((1,), (1,)))
    tiles = count // 8
    left = [gram[8 * t:8 * t + 8, :] for t in range(tiles)]
    right = [rows[8 * t:8 * t + 8, :] for t in range(tiles)]
    sub_left = lax.broadcasted_iota(jnp.int32, (8, count), 0)
    sub_right = lax.broadcasted_iota(jnp.int32, (8, width), 0)
    done = []
    for p in range(tiles):
        cols = [
            {t: jnp.broadcast_to(left[t][:, 8 * p + j:8 * p + j + 1], (8, width)) for t in range(p, tiles)}
            for j in range(8)
        ]
        scale = jnp.zeros((8, width), jnp.float32)
        for k in range(8):
            pivot = cols[k][p][k:k + 1, :]
            inverse = 1.0 / pivot
            scale = jnp.where(sub_right == k, lax.rsqrt(pivot), scale)
            row_left = left[p][k:k + 1, :] * inverse[:, :count]
            row_right = right[p][k:k + 1, :] * inverse
            row_cols = [cols[j][p][k:k + 1, :] * inverse for j in range(8)]
            for t in range(p, tiles):
                factor = cols[k][t]
                if t == p:
                    factor = jnp.where(sub_right > k, factor, 0.0)
                left[t] = left[t] - factor[:, :count] * row_left
                right[t] = right[t] - factor * row_right
                for j in range(k + 1, 8):
                    cols[j][t] = cols[j][t] - factor * row_cols[j]
        done.append(right[p] * scale)
    return jnp.concatenate(done, axis=0)


def z_kernel(rows_ref, block_ref, proj_ref, grams_ref):
    basis = orth_rows(rows_ref[...])
    proj_ref[...] = product3(basis, basis, ((0,), (0,)))
    none = jnp.zeros((64, 128), jnp.float32)
    pair = jnp.concatenate(
        [jnp.concatenate([basis, none], axis=1), jnp.concatenate([none, basis], axis=1)], axis=0
    )
    tiles = [block_ref[:, :, 8 * t:8 * t + 8, :].reshape(256, 128) for t in range(4)]
    wide = jnp.concatenate(
        [product3(jnp.concatenate(tiles[t:t + 2], axis=1), pair, ((1,), (1,))) for t in (0, 2)], axis=1
    )
    outer = product3(wide, wide, ((1,), (1,)))
    row = lax.broadcasted_iota(jnp.int32, (256, 256), 0)
    col = lax.broadcasted_iota(jnp.int32, (256, 256), 1)
    outer = jnp.where((row & 7) == (col & 7), outer, 0.0).reshape(32, 8, 256).sum(axis=1)
    fold = lax.broadcasted_iota(jnp.int32, (256, 32), 0) // 8
    fold = (fold == lax.broadcasted_iota(jnp.int32, (256, 32), 1)).astype(jnp.float32)
    gram = product(outer, fold, ((1,), (0,)))
    packed = jnp.concatenate([gram[8 * i:8 * i + 8] for i in range(4)], axis=1)
    for i in range(32):
        grams_ref[i] = packed


def v_kernel(grams_ref, factor_ref, proj_ref, rms_ref):
    total = grams_ref[0]
    for i in range(1, 32):
        total = total + grams_ref[i]
    gram = jnp.concatenate([total[:, 32 * i:32 * i + 32] for i in range(4)], axis=0)
    raw = product(factor_ref[...], gram, ((1,), (0,)))
    basis = orth_rows(raw)
    proj_ref[...] = product3(basis, basis, ((0,), (0,)))
    energy = jnp.sum(basis * product3(basis, gram, ((1,), (0,))), axis=(0, 1), keepdims=True)
    rms_ref[...] = jnp.sqrt(energy / (16 * 16 * 64 * 64))


def in_vmem(*shape):
    return pltpu.VMEM(shape, jnp.float32)


def fast(value):
    return pltpu.with_memory_space_constraint(value, pltpu.VMEM)


def slow(value):
    return pltpu.with_memory_space_constraint(value, pltpu.HBM)


def room(mib):
    return pltpu.CompilerParams(vmem_limit_bytes=mib << 20)


def whole():
    return pl.BlockSpec(memory_space=pltpu.VMEM)


def per_device(field, factor_x, factor_y, factor_z, factor_v):
    keep, send = pl.pallas_call(
        x_kernel,
        in_specs=[pl.BlockSpec(memory_space=pltpu.HBM)] * 3,
        out_specs=(whole(), whole()),
        out_shape=(in_vmem(8, 8, 32, 128), in_vmem(65, 32, 128)),
        scratch_shapes=[
            in_vmem(8, 32, 32, 128),
            in_vmem(16, 32),
            in_vmem(32, 64),
            pltpu.SemaphoreType.DMA((2,)),
            pltpu.SemaphoreType.DMA((2,)),
        ],
        compiler_params=room(12),
    )(slow(factor_x.T), slow(factor_y), slow(field))
    got = lax.ppermute(send, "c", swap)
    late_v, keep = lax.optimization_barrier((factor_v.T, keep))
    wide_v = pl.pallas_call(
        spread_kernel,
        in_specs=[whole()],
        out_specs=whole(),
        out_shape=in_vmem(128, 256),
        compiler_params=room(4),
    )(late_v)
    slots = pl.pallas_call(
        y_kernel,
        in_specs=[whole()] * 3,
        out_specs=whole(),
        out_shape=in_vmem(4, 4, 8, 32, 128),
        compiler_params=room(12),
    )(factor_y, fast(keep), fast(got))
    mine = gather_sum(gather_sum(slots, True), False)
    one, two, three = [
        lax.ppermute(mine, "x", [(i, (i + k) % 4) for i in range(4)]) for k in (1, 2, 3)
    ]
    raw, block = pl.pallas_call(
        raw_kernel,
        in_specs=[whole()] * 6,
        out_specs=(whole(), whole()),
        out_shape=(in_vmem(64, 128), in_vmem(4, 8, 32, 128)),
        compiler_params=room(12),
    )(fast(mine), fast(one), fast(two), fast(three), fast(wide_v), factor_z.T)
    raw = raw + lax.ppermute(raw, "c", swap)
    raw = sum_all(sum_all(raw, "y"), "z")
    proj_z, grams = pl.pallas_call(
        z_kernel,
        in_specs=[whole()] * 2,
        out_specs=(whole(), whole()),
        out_shape=(jax.ShapeDtypeStruct((128, 128), jnp.float32), in_vmem(32, 8, 128)),
        compiler_params=room(12),
    )(fast(raw), fast(block))
    grams = lax.all_to_all(grams, ("z", "y", "c"), 0, 0, tiled=True)
    proj_v, core_rms = pl.pallas_call(
        v_kernel,
        in_specs=[whole()] * 2,
        out_specs=(whole(), whole()),
        out_shape=(
            jax.ShapeDtypeStruct((32, 32), jnp.float32),
            jax.ShapeDtypeStruct((1, 1), jnp.float32),
        ),
        compiler_params=room(12),
    )(fast(grams), factor_v.T)
    return (proj_z, proj_v, core_rms[0, 0])


def solution(mesh):
    fine = Mesh(mesh.devices.reshape(4, 4, 2, 4), ("z", "y", "c", "x"))
    rows = ("z", "y", "c")
    in_specs = (P("x", None, rows, None), P(), P(rows, None), P(), P())
    out_specs = (P(), P(), P())
    return jax.shard_map(
        per_device, mesh=fine, in_specs=in_specs, out_specs=out_specs, check_vma=False
    )
```

```python
import jax
import jax.numpy as jnp
from jax import lax
from jax.experimental import pallas as pl
from jax.experimental.pallas import tpu as pltpu
from jax.sharding import Mesh, PartitionSpec as P

precise = lax.Precision.HIGHEST
swap = [(0, 1), (1, 0)]


def hops(step, first):
    pairs = []
    for z in range(4):
        for y in range(4):
            for c in range(2):
                along_y = (c == 0) == first
                to_z, to_y = (z, (y + step) % 4) if along_y else ((z + step) % 4, y)
                pairs.append((8 * z + 2 * y + c, 8 * to_z + 2 * to_y + c))
    return pairs


def gather_sum(slots, first):
    got = [lax.ppermute(slots[k], ("z", "y", "c"), hops(k, first)) for k in (2, 1, 3)]
    return (slots[0] + got[0]) + (got[1] + got[2])


def sum_all(value, axis):
    one, two, three = [
        lax.ppermute(value, axis, [(i, (i + k) % 4) for i in range(4)]) for k in (1, 2, 3)
    ]
    return (value + two) + (one + three)


def product(left, right, contract):
    return lax.dot_general(
        left, right, (contract, ((), ())), precision=precise,
        preferred_element_type=jnp.float32,
    )


def halves(value):
    high = value.astype(jnp.bfloat16)
    low = (value - high.astype(jnp.float32)).astype(jnp.bfloat16)
    return high, low


def product3(left, right, contract):
    (left_high, left_low), (right_high, right_low) = halves(left), halves(right)

    def one(a, b):
        return lax.dot_general(a, b, (contract, ((), ())), preferred_element_type=jnp.float32)

    return one(left_high, right_high) + (one(left_high, right_low) + one(left_low, right_high))


def dot16(left, right):
    return lax.dot_general(
        left, right, (((1,), (0,)), ((), ())), preferred_element_type=jnp.float32
    )


def spread(factor, turn):
    pick = lax.broadcasted_iota(jnp.int32, (128, 16), 0) // 8 + turn
    pick = jnp.where(pick >= 16, pick - 16, pick)
    pick = (pick == lax.broadcasted_iota(jnp.int32, (128, 16), 1)).astype(jnp.float32)
    wide = lax.broadcasted_iota(jnp.int32, (32, 256), 1) // 8
    wide = (wide == lax.broadcasted_iota(jnp.int32, (32, 256), 0)).astype(jnp.float32)
    full = product(product(pick, factor, ((1,), (0,))), wide, ((1,), (0,)))
    row = lax.broadcasted_iota(jnp.int32, (128, 256), 0)
    col = lax.broadcasted_iota(jnp.int32, (128, 256), 1)
    return jnp.where((row & 7) == (col & 7), full, 0.0)


def x_kernel(factor_ref, factor_y_ref, field_ref, keep_ref, send_ref, held, held_x, held_y, arrived, small):
    copies = [
        pltpu.make_async_copy(field_ref.at[low:high], held.at[low:high], arrived.at[i])
        for i, (low, high) in enumerate(((0, 3), (3, 8)))
    ]
    copy_x = pltpu.make_async_copy(factor_ref, held_x, small.at[0])
    copy_y = pltpu.make_async_copy(factor_y_ref, held_y, small.at[1])
    for copy in [copy_x, copy_y] + copies:
        copy.start()
    copy_x.wait()
    factor_high, factor_low = halves(spread(held_x[...], lax.axis_index("c") * 8))
    both = jnp.concatenate([factor_high, factor_low], axis=0)
    copy_y.wait()
    send_ref[64, :, 0:64] = held_y[...]
    send_ref[64, :, 64:128] = held_y[...]
    for v in range(8):
        if v in (0, 3):
            copies[v // 3].wait()
        tile = jnp.concatenate(
            [held[v, :, 8 * t:8 * t + 8, :].reshape(256, 128) for t in range(4)], axis=1
        )
        high, low = halves(tile)
        first = dot16(both, high)
        total = first[:128] + (first[128:] + dot16(factor_high, low))
        for t in range(4):
            cut = total[:, 128 * t:128 * t + 128].reshape(16, 8, 128)
            keep_ref[:, v, 8 * t:8 * t + 8, :] = cut[:8]
            for a in range(8):
                send_ref[8 * a + v, 8 * t:8 * t + 8, :] = cut[8 + a]


def y_kernel(mine_ref, keep_ref, got_ref, slots_ref):
    my_y, my_z, core = lax.axis_index("y"), lax.axis_index("z"), lax.axis_index("c")
    high, low = halves(jnp.concatenate([mine_ref[...], got_ref[64, :, 0:64]], axis=0).T)
    left = jnp.concatenate([high, low, high], axis=1)
    for a in range(8):
        tile = jnp.concatenate(
            [jnp.concatenate([keep_ref[a, v], got_ref[8 * a + v]], axis=0) for v in range(8)], axis=1
        )
        high, low = halves(tile)
        total = dot16(left, jnp.concatenate([high, high, low], axis=0))
        for half in range(2):
            to_z, to_y = divmod(2 * a + half, 4)
            dz, dy = (to_z - my_z + 4) % 4, (to_y - my_y + 4) % 4
            first = dy + core * (dz - dy)
            second = dz + core * (dy - dz)
            for v in range(8):
                slots_ref[first, second, v] = total[32 * half:32 * half + 32, 128 * v:128 * v + 128]


def spread_kernel(factor_ref, spread_ref):
    spread_ref[...] = spread(factor_ref[...], 0)


def raw_kernel(mine_ref, one_ref, two_ref, three_ref, spread_ref, factor_z_ref, raw_ref, block_ref):
    my_x = lax.axis_index("x")
    for back, ref in enumerate((mine_ref, one_ref, two_ref, three_ref)):
        block_ref[(my_x - back + 4) % 4] = ref[...]
    left = spread_ref[...]
    tile = jnp.concatenate(
        [block_ref[:, :, 8 * t:8 * t + 8, :].reshape(256, 128) for t in range(4)], axis=1
    )
    wide = product3(left, tile, ((1,), (0,)))
    wide = jnp.concatenate([wide[:, 128 * t:128 * t + 128] for t in range(4)], axis=0)
    small = product3(wide, factor_z_ref[...], ((1,), (1,)))
    raw_ref[...] = product3(small, wide, ((0,), (0,)))


def orth_rows(rows):
    count, width = rows.shape
    gram = product(rows, rows, ((1,), (1,)))
    tiles = count // 8
    left = [gram[8 * t:8 * t + 8, :] for t in range(tiles)]
    right = [rows[8 * t:8 * t + 8, :] for t in range(tiles)]
    sub_left = lax.broadcasted_iota(jnp.int32, (8, count), 0)
    sub_right = lax.broadcasted_iota(jnp.int32, (8, width), 0)
    done = []
    for p in range(tiles):
        cols = [
            {t: jnp.broadcast_to(left[t][:, 8 * p + j:8 * p + j + 1], (8, width)) for t in range(p, tiles)}
            for j in range(8)
        ]
        scale = jnp.zeros((8, width), jnp.float32)
        for k in range(8):
            pivot = cols[k][p][k:k + 1, :]
            inverse = 1.0 / pivot
            scale = jnp.where(sub_right == k, lax.rsqrt(pivot), scale)
            row_left = left[p][k:k + 1, :] * inverse[:, :count]
            row_right = right[p][k:k + 1, :] * inverse
            row_cols = [cols[j][p][k:k + 1, :] * inverse for j in range(8)]
            for t in range(p, tiles):
                factor = cols[k][t]
                if t == p:
                    factor = jnp.where(sub_right > k, factor, 0.0)
                left[t] = left[t] - factor[:, :count] * row_left
                right[t] = right[t] - factor * row_right
                for j in range(k + 1, 8):
                    cols[j][t] = cols[j][t] - factor * row_cols[j]
        done.append(right[p] * scale)
    return jnp.concatenate(done, axis=0)


def z_kernel(rows_ref, block_ref, proj_ref, grams_ref):
    basis = orth_rows(rows_ref[...])
    proj_ref[...] = product3(basis, basis, ((0,), (0,)))
    none = jnp.zeros((64, 128), jnp.float32)
    pair = jnp.concatenate(
        [jnp.concatenate([basis, none], axis=1), jnp.concatenate([none, basis], axis=1)], axis=0
    )
    tiles = [block_ref[:, :, 8 * t:8 * t + 8, :].reshape(256, 128) for t in range(4)]
    wide = jnp.concatenate(
        [product3(jnp.concatenate(tiles[t:t + 2], axis=1), pair, ((1,), (1,))) for t in (0, 2)], axis=1
    )
    outer = product3(wide, wide, ((1,), (1,)))
    row = lax.broadcasted_iota(jnp.int32, (256, 256), 0)
    col = lax.broadcasted_iota(jnp.int32, (256, 256), 1)
    outer = jnp.where((row & 7) == (col & 7), outer, 0.0).reshape(32, 8, 256).sum(axis=1)
    fold = lax.broadcasted_iota(jnp.int32, (256, 32), 0) // 8
    fold = (fold == lax.broadcasted_iota(jnp.int32, (256, 32), 1)).astype(jnp.float32)
    gram = product(outer, fold, ((1,), (0,)))
    packed = jnp.concatenate([gram[8 * i:8 * i + 8] for i in range(4)], axis=1)
    for i in range(32):
        grams_ref[i] = packed


def v_kernel(grams_ref, factor_ref, proj_ref, rms_ref):
    total = grams_ref[0]
    for i in range(1, 32):
        total = total + grams_ref[i]
    gram = jnp.concatenate([total[:, 32 * i:32 * i + 32] for i in range(4)], axis=0)
    raw = product(factor_ref[...], gram, ((1,), (0,)))
    basis = orth_rows(raw)
    proj_ref[...] = product3(basis, basis, ((0,), (0,)))
    energy = jnp.sum(basis * product3(basis, gram, ((1,), (0,))), axis=(0, 1), keepdims=True)
    rms_ref[...] = jnp.sqrt(energy / (16 * 16 * 64 * 64))


def in_vmem(*shape):
    return pltpu.VMEM(shape, jnp.float32)


def fast(value):
    return pltpu.with_memory_space_constraint(value, pltpu.VMEM)


def slow(value):
    return pltpu.with_memory_space_constraint(value, pltpu.HBM)


def room(mib):
    return pltpu.CompilerParams(vmem_limit_bytes=mib << 20)


def whole():
    return pl.BlockSpec(memory_space=pltpu.VMEM)


def per_device(field, factor_x, factor_y, factor_z, factor_v):
    keep, send = pl.pallas_call(
        x_kernel,
        in_specs=[pl.BlockSpec(memory_space=pltpu.HBM)] * 3,
        out_specs=(whole(), whole()),
        out_shape=(in_vmem(8, 8, 32, 128), in_vmem(65, 32, 128)),
        scratch_shapes=[
            in_vmem(8, 32, 32, 128),
            in_vmem(16, 32),
            in_vmem(32, 64),
            pltpu.SemaphoreType.DMA((2,)),
            pltpu.SemaphoreType.DMA((2,)),
        ],
        compiler_params=room(12),
    )(slow(factor_x.T), slow(factor_y), slow(field))
    got = lax.ppermute(send, "c", swap)
    late_v, keep = lax.optimization_barrier((factor_v.T, keep))
    wide_v = pl.pallas_call(
        spread_kernel,
        in_specs=[whole()],
        out_specs=whole(),
        out_shape=in_vmem(128, 256),
        compiler_params=room(4),
    )(late_v)
    slots = pl.pallas_call(
        y_kernel,
        in_specs=[whole()] * 3,
        out_specs=whole(),
        out_shape=in_vmem(4, 4, 8, 32, 128),
        compiler_params=room(12),
    )(factor_y, fast(keep), fast(got))
    mine = gather_sum(gather_sum(slots, True), False)
    one, two, three = [
        lax.ppermute(mine, "x", [(i, (i + k) % 4) for i in range(4)]) for k in (1, 2, 3)
    ]
    raw, block = pl.pallas_call(
        raw_kernel,
        in_specs=[whole()] * 6,
        out_specs=(whole(), whole()),
        out_shape=(in_vmem(64, 128), in_vmem(4, 8, 32, 128)),
        compiler_params=room(12),
    )(fast(mine), fast(one), fast(two), fast(three), fast(wide_v), factor_z.T)
    raw = raw + lax.ppermute(raw, "c", swap)
    raw = sum_all(sum_all(raw, "y"), "z")
    proj_z, grams = pl.pallas_call(
        z_kernel,
        in_specs=[whole()] * 2,
        out_specs=(whole(), whole()),
        out_shape=(jax.ShapeDtypeStruct((128, 128), jnp.float32), in_vmem(32, 8, 128)),
        compiler_params=room(12),
    )(fast(raw), fast(block))
    grams = lax.all_to_all(grams, ("z", "y", "c"), 0, 0, tiled=True)
    proj_v, core_rms = pl.pallas_call(
        v_kernel,
        in_specs=[whole()] * 2,
        out_specs=(whole(), whole()),
        out_shape=(
            jax.ShapeDtypeStruct((32, 32), jnp.float32),
            jax.ShapeDtypeStruct((1, 1), jnp.float32),
        ),
        compiler_params=room(12),
    )(fast(grams), factor_v.T)
    return (proj_z, proj_v, core_rms[0, 0])


def solution(mesh):
    fine = Mesh(mesh.devices.reshape(4, 4, 2, 4), ("z", "y", "c", "x"))
    rows = ("z", "y", "c")
    in_specs = (P("x", None, rows, None), P(), P(rows, None), P(), P())
    out_specs = (P(), P(), P())
    return jax.shard_map(
        per_device, mesh=fine, in_specs=in_specs, out_specs=out_specs, check_vma=False
    )
```
